32 devices in a mesh: row: 8 (over y, x, core), col: 4 (over z).
Axes of the slice: x: 2, y: 2, z: 4, core: 2. Of those that a mesh axis runs over, the one named last changes fastest.
Arguments:
- x_mat: float32 [512, 512], replicated, may hold values from -8 to 40, as said below
- y_inv: float32 [512, 512], replicated, may hold values from -8 to 40, as said below
- panel_blocks: bfloat16 [512, 4096], replicated, may hold values from -6 to 6
- panel_pos: int32 [512], replicated, may hold values from 0 to 63
- group_blocks: int32 [32, 2], replicated, may hold values from 0 to 63
- cons_blocks: bfloat16 [57344, 4096], P(('row', 'col')), may hold values from -6 to 6
- slot_block: int32 [57344], P(('row', 'col')), may hold values from 0 to 1
- slot_row: int32 [57344], P(('row', 'col')), may hold values from 0 to 32767, as said below
- group_size: int32 [32], P(('row', 'col')), may hold values from 768 to 1792, as said below
- trailing: float32 [32768, 2048], P('row', 'col'), may hold values from -6 to 6
Outputs:
- lower_panel: float32 [32768, 512], P(('row', 'col'))
- updated: float32 [32768, 2048], P('row', 'col')
The draws below stay inside these ranges and needn't reach their ends.
Inputs may be any that keep to these rules, and one draw needn't show every extreme that they name: `x_mat`: symmetric positive definite. `y_inv`: symmetric positive definite. `slot_row`: over all groups, the live slots hold every row 0 to 32767 exactly once; the live slots of one group hold at most 56 rows of one aligned range of 1024 rows, and that most is reached in every draw; other slots hold arbitrary rows. `group_size`: the live slots of a group are its first slots; some group has exactly 1792 in every draw.
All inputs are finite; a program needn't handle non-finite values.
Results may differ from the reference program's by a relative error of at most 0.004.
Values may be sent and summed in bfloat16 or wider, within the bound.
A program may use at most 192 MiB of HBM per device.

```python
import math
import jax
import jax.numpy as jnp
from jax import lax

N = 512
BS = 64
NB = 8
PANEL = 512
TRAIL = 2048
CAP = 2
ROWS_DEV = 4096
M2 = 32768
SUB = 1024
CS = 1792
RB = 64
N_ROW = 8
N_COL = 4
DEVICES = 32


def spd_matrix(key, salt):
    key_one = jax.random.fold_in(jax.random.fold_in(key, salt), 0)
    base = jax.random.normal(key_one, (N, N), jnp.float32)
    gram = jnp.dot(base, base.T, precision=lax.Precision.HIGHEST) / N
    return gram + 0.3 * jnp.eye(N, dtype=jnp.float32)


def draw_x_mat(key, part):
    return spd_matrix(key, 3)


def draw_y_inv(key, part):
    return spd_matrix(key, 5)


def slot_layout(key):
    devices = N_ROW * N_COL
    base_share = SUB // devices
    spread = SUB - devices // 4 * base_share
    key_list = jax.random.split(jax.random.fold_in(key, 11), 5)
    heavy_part = jax.random.permutation(key_list[0], jnp.where(jnp.arange(devices) < devices // 4, base_share, 0).astype(jnp.int32))
    extra_part = jax.random.permutation(key_list[1], (spread // devices + (jnp.arange(devices) < spread % devices).astype(jnp.int32)).astype(jnp.int32))
    source_ids = jnp.arange(devices)[:, None]
    dest_ids = jnp.arange(devices)[None, :]
    counts = heavy_part[:, None] + extra_part[(source_ids + dest_ids) % devices]
    recv_start = jnp.cumsum(counts, axis=0) - counts
    orders = jax.vmap(lambda sub_key: jax.random.permutation(sub_key, SUB))(jax.random.split(key_list[2], devices))
    send_end = jnp.cumsum(counts, axis=1)
    send_start = send_end - counts
    group_total = send_end[:, -1]
    slot_ids = jnp.arange(CS, dtype=jnp.int32)
    dest_of = jax.vmap(lambda ends: jnp.searchsorted(ends, slot_ids, side='right'))(send_end)
    dest_clip = jnp.minimum(dest_of, devices - 1).astype(jnp.int32)
    offset = slot_ids[None, :] - jnp.take_along_axis(send_start, dest_clip, axis=1)
    local_pos = jnp.clip(jnp.take_along_axis(recv_start, dest_clip, axis=1) + offset, 0, SUB - 1)
    local_row = orders[dest_clip, local_pos]
    live_slots = slot_ids[None, :] < group_total[:, None]
    dead_rows = jax.random.randint(key_list[3], (devices, CS), 0, M2)
    row_ids = jnp.where(live_slots, dest_clip * SUB + local_row, dead_rows)
    sort_key = jax.random.randint(key_list[4], (devices, CS), 0, 1 << 20) + jnp.where(live_slots, 0, 1 << 21)
    shuffle = jnp.argsort(sort_key, axis=1, stable=True)
    row_ids = jnp.take_along_axis(row_ids, shuffle, axis=1)
    return (row_ids.reshape(-1).astype(jnp.int32), group_total.astype(jnp.int32))


def draw_slot_row(key, part):
    return slot_layout(key)[0]


def draw_group_size(key, part):
    return slot_layout(key)[1]


def set_ends(result, rng, smallest, high):
    dims = result.shape
    place = [jax.random.randint(jax.random.fold_in(rng, axis), (), 0, dims[axis]) for axis in range(len(dims))]
    result = result.at[tuple(place)].set(smallest)
    longest = dims.index(max(dims))
    place[longest] = (place[longest] + 1) % dims[longest]
    return result.at[tuple(place)].set(high)


def block_levels(own_key, extent, cuts, smallest, high):
    def one(dim, blocks):
        heights = jax.random.uniform(jax.random.fold_in(jax.random.fold_in(own_key, 6), dim), (blocks,), jnp.float32, smallest / len(cuts), high / len(cuts))
        return jnp.repeat(jnp.exp(heights), extent[dim] // blocks).reshape((-1,) + (1,) * (len(extent) - dim - 1))

    loudness = one(*cuts[0])
    for cut in cuts[1:]:
        loudness = loudness * one(*cut)
    return loudness


def normal_values(key, shape, scale, bound, cuts=(), kind=jnp.bfloat16):
    result = jax.random.normal(key, shape, jnp.float32) * scale
    if len(cuts) > 0:
        result = block_levels(key, shape, cuts, -0.22, 0.18) * result
    return jnp.clip(result, min=-bound, max=bound).astype(kind)


def setup_inputs(seed: int = 0) -> dict:
    seeds = jax.random.split(jax.random.key(seed), 11)
    return {
        "x_mat": draw_x_mat(jax.random.fold_in(seeds[10], 71), 0),
        "y_inv": draw_y_inv(jax.random.fold_in(seeds[10], 71), 0),
        "panel_blocks": normal_values(seeds[2], (PANEL, BS * BS), 1.0, 6.0),
        "panel_pos": set_ends(jax.random.randint(seeds[3], (PANEL,), 0, NB * NB), jax.random.fold_in(seeds[3], 1), 0, (NB * NB) - 1).astype(jnp.int32),
        "group_blocks": set_ends(jax.random.randint(seeds[4], (DEVICES, CAP), 0, NB * NB), jax.random.fold_in(seeds[4], 1), 0, (NB * NB) - 1).astype(jnp.int32),
        "cons_blocks": normal_values(seeds[5], (DEVICES * CS, BS * BS), 1.0, 6.0, ((0, 32),)),
        "slot_block": set_ends(jax.random.randint(seeds[6], (DEVICES * CS,), 0, CAP), jax.random.fold_in(seeds[6], 1), 0, CAP - 1).astype(jnp.int32),
        "slot_row": draw_slot_row(jax.random.fold_in(seeds[10], 71), 0),
        "group_size": draw_group_size(jax.random.fold_in(seeds[10], 71), 0),
        "trailing": normal_values(seeds[9], (M2, TRAIL), 1.0, 6.0, ((0, 8), (1, 4)), jnp.float32),
    }


def build_h(values, position, x_mat, y_inv):
    highest = lax.Precision.HIGHEST
    matrix_order = x_mat.shape[0]
    block_size = math.isqrt(values.shape[0])
    block_count = matrix_order // block_size
    e_mat = values.reshape(block_size, block_size).astype(jnp.float32)
    row_start = position // block_count * block_size
    col_start = position % block_count * block_size
    x_left = lax.dynamic_slice_in_dim(x_mat, row_start, block_size, 1)
    x_right = lax.dynamic_slice_in_dim(x_mat, col_start, block_size, 1)
    y_low = lax.dynamic_slice_in_dim(y_inv, col_start, block_size, 0)
    y_high = lax.dynamic_slice_in_dim(y_inv, row_start, block_size, 0)
    term_one = jnp.dot(jnp.dot(x_left, e_mat, precision=highest), y_low, precision=highest)
    term_two = jnp.dot(jnp.dot(x_right, e_mat.T, precision=highest), y_high, precision=highest)
    g_mat = term_one + term_two
    h_mat = (g_mat + g_mat.T).astype(jnp.bfloat16)
    h_mat = h_mat.reshape(block_count, block_size, block_count, block_size).transpose(0, 2, 1, 3)
    return h_mat.reshape(block_count * block_count, block_size * block_size)

def reference(x_mat, y_inv, panel_blocks, panel_pos, group_blocks, cons_blocks, slot_block, slot_row, group_size, trailing):
    highest = lax.Precision.HIGHEST
    devices = N_ROW * N_COL
    blocks_all = lax.map(lambda pair_item: build_h(pair_item[0], pair_item[1], x_mat, y_inv), (panel_blocks, panel_pos))
    panel_float = panel_blocks.astype(jnp.float32)

    def diag_column(blocks_one):
        chosen = jnp.take(blocks_one, panel_pos, axis=0).astype(jnp.float32)
        return lax.optimization_barrier(jnp.sum(panel_float * chosen, axis=1))
    panel_schur = lax.map(diag_column, blocks_all).T
    symmetric = 0.5 * (panel_schur + panel_schur.T)
    diag_shift = 0.01 * jnp.mean(jnp.diagonal(symmetric))
    factor = jnp.linalg.cholesky(symmetric + diag_shift * jnp.eye(PANEL, dtype=jnp.float32))

    def device_rows(dev_item):
        cons_dev, blocks_dev, which_dev = dev_item
        cons_float = cons_dev.astype(jnp.float32)
        running = jnp.zeros((CS, PANEL), jnp.float32)
        for slot_index in range(CAP):
            table = jnp.take(blocks_all, blocks_dev[slot_index], axis=1).astype(jnp.float32)
            product_part = jnp.dot(cons_float, table.T, precision=highest)
            running = jnp.where((which_dev == slot_index)[:, None], product_part, running)
        return running
    rows_all = lax.map(device_rows, (cons_blocks.reshape(devices, CS, BS * BS), group_blocks, slot_block.reshape(devices, CS)))
    live_slots = jnp.arange(CS, dtype=jnp.int32)[None, :] < group_size[:, None]
    target = jnp.where(live_slots, slot_row.reshape(devices, CS), M2).astype(jnp.int32)
    row_schur = jnp.zeros((M2, PANEL), jnp.float32).at[target.reshape(-1)].set(rows_all.reshape(-1, PANEL), mode='drop')
    lower_panel = lax.linalg.triangular_solve(factor, row_schur, left_side=False, lower=True, transpose_a=True)
    col_ids = jnp.arange(TRAIL, dtype=jnp.int32)
    source = col_ids // RB % N_ROW * ROWS_DEV + col_ids // (RB * N_ROW) * RB + col_ids % RB
    picked = jnp.take(lower_panel, source.astype(jnp.int32), axis=0)
    updated = trailing - jnp.dot(lower_panel, picked.T, precision=highest)
    return (lower_panel, updated)
```

```python
import functools
import math

import jax
import jax.numpy as jnp
from jax import lax
from jax.experimental import pallas as pl
from jax.experimental.pallas import tpu as pltpu
from jax.sharding import PartitionSpec as P

BF16 = jnp.bfloat16
F32 = jnp.float32


def split(value):
    high = value.astype(BF16)
    low = (value - high.astype(F32)).astype(BF16)
    return high, low


def halves(block_size, rows):
    return lax.broadcasted_iota(jnp.int32, (rows, 2 * block_size), 1) < block_size


def congruence(p, q, pair, left_ref, high_ref, low_ref):
    block_size = pair.shape[0]
    keep = halves(block_size, block_size)
    zero = jnp.zeros_like(pair)
    first = jnp.where(keep, pair, zero)
    second = jnp.where(keep, zero, pair)
    stacked = jnp.concatenate([first, first, second, second], axis=0)
    left = jnp.concatenate([left_ref[p], left_ref[q]], axis=1)
    inner = jnp.dot(left, stacked, preferred_element_type=F32)
    rows = inner.shape[0] // 2
    wide = jnp.concatenate([inner[:rows], inner[rows:]], axis=1)
    wide_high, wide_low = split(wide)
    z_high = jnp.concatenate([high_ref[0, q], high_ref[0, p], high_ref[1, q], high_ref[1, p]], axis=0)
    z_low = jnp.concatenate([low_ref[0, q], low_ref[0, p], low_ref[1, q], low_ref[1, p]], axis=0)
    dot = functools.partial(jnp.dot, preferred_element_type=F32)
    return dot(wide_high, z_high) + (dot(wide_high, z_low) + dot(wide_low, z_high))


def own_kernel(block_count, pos_ref, pair_ref, left_ref, high_ref, low_ref, out_ref, scr):
    step = pl.program_id(0)
    position = pos_ref[step]
    p = position // block_count
    q = position % block_count
    h = congruence(p, q, pair_ref[0], left_ref, high_ref, low_ref)
    order = h.shape[0]
    block_size = order // block_count
    lanes = 2 * block_size
    groups = order // lanes
    for g in range(groups):
        scr[g * order : (g + 1) * order, :] = h[:, g * lanes : (g + 1) * lanes]
    keep = halves(block_size, block_count)
    for g in range(groups):
        for r in range(0, block_size, 2):
            even = scr[pl.ds(g * order + r, block_count, stride=block_size), :]
            odd = scr[pl.ds(g * order + r + 1, block_count, stride=block_size), :]
            one = jnp.where(keep, even, pltpu.roll(odd, block_size, 1))
            two = jnp.where(keep, pltpu.roll(even, block_size, 1), odd)
            both = jnp.concatenate([one, two], axis=0).astype(BF16)
            out_ref[
                2 * g * block_count : 2 * (g + 1) * block_count,
                r * block_size : (r + 2) * block_size,
            ] = both


def group_kernel(block_count, tile, pos_ref, pair_ref, left_ref, high_ref, low_ref, out_ref, scr):
    step = pl.program_id(0)
    block_size = pair_ref.shape[1]
    keep_rows = halves(block_size, block_size)
    for j in range(tile):
        position = pos_ref[step * tile + j]
        p = position // block_count
        q = position % block_count
        h = congruence(p, q, pair_ref[j], left_ref, high_ref, low_ref)
        scr[j * block_size : (j + 1) * block_size, :] = jnp.where(
            keep_rows, h[:block_size], h[block_size:]
        )
    keep = halves(block_size, tile)
    for r in range(0, block_size, 2):
        even = scr[pl.ds(r, tile, stride=block_size), :]
        odd = scr[pl.ds(r + 1, tile, stride=block_size), :]
        columns = slice(r * block_size, (r + 2) * block_size)
        out_ref[0, :, columns] = jnp.where(keep, even, pltpu.roll(odd, block_size, 1)).astype(BF16)
        out_ref[1, :, columns] = jnp.where(keep, pltpu.roll(even, block_size, 1), odd).astype(BF16)


def whole(shape):
    return pl.BlockSpec(shape, lambda *_: (0,) * len(shape))


def own_table(pairs, positions, left, high, low, block_count):
    count, block_size, lanes = pairs.shape
    order = block_count * block_size
    rows = block_count * block_count
    return pl.pallas_call(
        functools.partial(own_kernel, block_count),
        grid_spec=pltpu.PrefetchScalarGridSpec(
            num_scalar_prefetch=1,
            grid=(count,),
            in_specs=[
                pl.BlockSpec((1, block_size, lanes), lambda i, _: (i, 0, 0)),
                whole(left.shape),
                whole(high.shape),
                whole(low.shape),
            ],
            out_specs=pl.BlockSpec((rows, block_size * block_size), lambda i, _: (i, 0)),
            scratch_shapes=[pltpu.VMEM((order * order // lanes, lanes), F32)],
        ),
        out_shape=jax.ShapeDtypeStruct((count * rows, block_size * block_size), BF16),
        name="own_table",
    )(positions, pairs, left, high, low)


def group_table(pairs, positions, left, high, low, block_count):
    count, block_size, lanes = pairs.shape
    tile = 16
    return pl.pallas_call(
        functools.partial(group_kernel, block_count, tile),
        grid_spec=pltpu.PrefetchScalarGridSpec(
            num_scalar_prefetch=1,
            grid=(count // tile,),
            in_specs=[
                pl.BlockSpec((tile, block_size, lanes), lambda i, _: (i, 0, 0)),
                whole(left.shape),
                whole(high.shape),
                whole(low.shape),
            ],
            out_specs=pl.BlockSpec((2, tile, block_size * block_size), lambda i, _: (0, i, 0)),
            scratch_shapes=[pltpu.VMEM((tile * block_size, lanes), F32)],
        ),
        out_shape=jax.ShapeDtypeStruct((2, count, block_size * block_size), BF16),
        cost_estimate=pl.CostEstimate(
            flops=40 * 10**9, bytes_accessed=20 * 10**6, transcendentals=0
        ),
        name="group_table",
    )(positions, pairs, left, high, low)


def hdot(a, b, contract):
    return lax.dot_general(
        a, b, ((contract[:1], contract[1:]), ((), ())),
        precision=lax.Precision.HIGHEST, preferred_element_type=F32,
    )


def factor_kernel(block, s_ref, out_ref, a, work):
    order = s_ref.shape[0]
    count = order // block
    groups = block // 8
    a[...] = s_ref[...]
    row_id = lax.broadcasted_iota(jnp.int32, (8, 1), 0)
    eye = (
        lax.broadcasted_iota(jnp.int32, (block, block), 0)
        == lax.broadcasted_iota(jnp.int32, (block, block), 1)
    ).astype(F32)

    def diagonal(b, carry):
        start = pl.multiple_of(b * block, block)
        work[:, :block] = a[pl.ds(start, block), pl.ds(start, block)]
        work[:, block:] = eye
        rows = [work[8 * g : 8 * g + 8, :] for g in range(groups)]
        for k in range(block):
            g, s = divmod(k, 8)
            pivot_row = rows[g][s : s + 1, :]
            d = pivot_row[:, k : k + 1]
            inv = lax.rsqrt(d)
            inv = inv * (1.5 - 0.5 * d * inv * inv)
            scaled = pivot_row * inv
            for i in range(g, groups):
                mult = rows[i][:, k : k + 1] * inv
                if i == g:
                    mult = jnp.where(row_id > s, mult, 0.0)
                    rows[i] = jnp.where(row_id == s, scaled, rows[i] - mult * scaled)
                else:
                    rows[i] = rows[i] - mult * scaled
        inverse = jnp.concatenate([row[:, block:] for row in rows], axis=0)
        out_ref[pl.ds(start, block), pl.ds(start, block)] = inverse
        panel = hdot(a[:, pl.ds(start, block)], inverse, (1, 1))
        below = lax.broadcasted_iota(jnp.int32, (order, 1), 0) >= start + block
        panel = jnp.where(below, panel, 0.0)
        a[:, pl.ds(start, block)] = panel
        return carry, panel

    def body(b, carry):
        _, panel = diagonal(b, carry)
        start = pl.multiple_of(b * block, block)

        for i in range(1, count):
            @pl.when(b < i)
            def _():
                piece = a[i * block : (i + 1) * block, pl.ds(start, block)]
                cols = slice(i * block, (i + 1) * block)
                a[:, cols] = a[:, cols] - hdot(panel, piece, (1, 1))

        return carry

    lax.fori_loop(0, count, body, 0)
    for i in range(count):
        for b in range(i + 1, count):
            out_ref[i * block : (i + 1) * block, b * block : (b + 1) * block] = jnp.zeros(
                (block, block), F32
            )
    for i in range(1, count):
        low_row = a[i * block : (i + 1) * block, : i * block]
        total = hdot(low_row, out_ref[: i * block, : i * block], (1, 0))
        own = out_ref[i * block : (i + 1) * block, i * block : (i + 1) * block]
        out_ref[i * block : (i + 1) * block, : i * block] = -hdot(own, total, (1, 0))


def inverse_factor(matrix):
    order = matrix.shape[0]
    block = 128
    return pl.pallas_call(
        functools.partial(factor_kernel, block),
        in_specs=[pl.BlockSpec(memory_space=pltpu.VMEM)],
        out_specs=pl.BlockSpec(memory_space=pltpu.VMEM),
        out_shape=jax.ShapeDtypeStruct((order, order), F32),
        scratch_shapes=[pltpu.VMEM((order, order), F32), pltpu.VMEM((block, 2 * block), F32)],
        cost_estimate=pl.CostEstimate(
            flops=60 * 10**9, bytes_accessed=2 * 10**6, transcendentals=order
        ),
        name="inverse_factor",
    )(matrix)


def blocks_of_columns(matrix, block_count):
    rows = matrix.shape[0]
    return matrix.reshape(rows, block_count, -1).transpose(1, 0, 2)


def body(
    x_mat,
    y_inv,
    panel_blocks,
    panel_pos,
    group_blocks,
    cons_blocks,
    slot_block,
    slot_row,
    group_size,
    trailing,
):
    rows_size = lax.axis_size("row")
    cols_size = lax.axis_size("col")
    devices = rows_size * cols_size
    col_index = lax.axis_index("col")
    device_id = lax.axis_index("row") * cols_size + col_index
    panel_cols = panel_blocks.shape[0]
    per_device = panel_cols // devices
    order = x_mat.shape[0]
    block_size = math.isqrt(panel_blocks.shape[1])
    block_count = order // block_size
    square = panel_blocks.reshape(panel_cols, block_size, block_size)
    pairs = jnp.concatenate([square, square.transpose(0, 2, 1)], axis=2)
    both = jnp.stack([y_inv, x_mat])
    rounded = lax.reduce_precision(both, exponent_bits=8, mantissa_bits=7)
    both_high = rounded.astype(BF16)
    both_low = lax.reduce_precision(both - rounded, exponent_bits=8, mantissa_bits=7).astype(BF16)
    high = both_high.reshape(2, block_count, block_size, order)
    low = both_low.reshape(2, block_count, block_size, order)
    tall_high = jnp.concatenate([both_high[1], both_high[0]], axis=0)
    tall_low = jnp.concatenate([both_low[1], both_low[0]], axis=0)
    left = jnp.concatenate(
        [blocks_of_columns(tall_high, block_count), blocks_of_columns(tall_low, block_count)], axis=2
    )
    own_pairs = lax.dynamic_slice_in_dim(pairs, device_id * per_device, per_device, 0)
    own_pos = lax.dynamic_slice_in_dim(panel_pos, device_id * per_device, per_device, 0)
    own_rows = own_table(own_pairs, own_pos, left, high, low, block_count)
    products = lax.dot_general(
        own_rows, panel_blocks, (((1,), (1,)), ((), ())), preferred_element_type=F32
    )
    place = panel_pos % block_count * block_count + panel_pos // block_count
    position_count = block_count * block_count
    hit = jnp.arange(position_count, dtype=jnp.int32)[:, None] == place[None, :]
    row_part = jnp.sum(
        jnp.where(hit[None], products.reshape(per_device, position_count, panel_cols), 0.0), axis=1
    )
    panel_schur = lax.all_gather(row_part, ("row", "col"), axis=0, tiled=True)

    own_group = lax.dynamic_index_in_dim(group_blocks, device_id, 0, keepdims=False)
    slots = own_group.shape[0]
    lefts, highs, lows = [], [], []
    for slot_index in range(slots):
        a_block = own_group[slot_index] // block_count
        b_start = own_group[slot_index] % block_count * block_size
        lefts.append(
            lax.dynamic_slice_in_dim(
                left.reshape(block_count, 2, order, 2 * block_size), a_block * block_size, block_size, 2
            )
        )
        highs.append(lax.dynamic_slice_in_dim(high, b_start, block_size, 3))
        lows.append(lax.dynamic_slice_in_dim(low, b_start, block_size, 3))
    group_left = jnp.concatenate(lefts, axis=2).reshape(
        block_count, 2 * slots * block_size, 2 * block_size
    )
    group_rows = group_table(
        pairs, panel_pos, group_left, jnp.concatenate(highs, axis=3), jnp.concatenate(lows, axis=3),
        block_count,
    )
    slot_count = cons_blocks.shape[0]
    running = None
    for slot_index in range(slots):
        product_part = lax.dot_general(
            cons_blocks, group_rows[slot_index], (((1,), (1,)), ((), ())), preferred_element_type=F32
        )
        if running is None:
            running = jnp.where((slot_block == slot_index)[:, None], product_part, 0.0)
        else:
            running = jnp.where((slot_block == slot_index)[:, None], product_part, running)
    schur_rows = running

    sub_rows = trailing.shape[0] // cols_size
    base_share = sub_rows // devices
    spread = sub_rows - devices // 4 * base_share
    capacity = base_share + (spread + devices - 1) // devices
    live_slots = jnp.arange(slot_count, dtype=jnp.int32) < group_size[0]
    target = slot_row // sub_rows
    dest_hits = (
        (target[:, None] == jnp.arange(devices, dtype=jnp.int32)[None, :]) & live_slots[:, None]
    ).astype(jnp.int32)
    before = jnp.cumsum(dest_hits, axis=0) - dest_hits
    dest_rank = jnp.sum(before * dest_hits, axis=1)
    slot_place = jnp.where(live_slots, target * capacity + dest_rank, devices * capacity)
    place_ids = jnp.arange(devices * capacity, dtype=jnp.int32)
    send_hits = (place_ids[:, None] == slot_place[None, :]).astype(BF16)
    send_rows = jnp.dot(
        send_hits, schur_rows.astype(BF16), preferred_element_type=F32
    ).astype(BF16)
    send_local = (
        jnp.full((devices * capacity,), sub_rows, jnp.int32)
        .at[slot_place]
        .set(slot_row % sub_rows, mode="drop")
    )
    exchange = functools.partial(
        lax.all_to_all, axis_name=("row", "col"), split_axis=0, concat_axis=0, tiled=True
    )
    recv_local = exchange(send_local.reshape(devices, capacity))
    recv_rows = exchange(send_rows.reshape(devices, capacity, panel_cols))
    symmetric = 0.5 * (panel_schur + panel_schur.T)
    diag_shift = 0.01 * jnp.mean(jnp.diagonal(symmetric))
    inverse = inverse_factor(symmetric + diag_shift * jnp.eye(panel_cols, dtype=F32))
    local_ids = jnp.arange(sub_rows, dtype=jnp.int32)
    recv_hits = (local_ids[:, None] == recv_local.reshape(1, -1)).astype(BF16)
    row_slab = jnp.dot(
        recv_hits, recv_rows.reshape(-1, panel_cols), preferred_element_type=F32
    )
    lower_slab = hdot(row_slab, inverse, (1, 1))
    all_rows = lax.all_gather(lower_slab.astype(BF16), "col", axis=0, tiled=True)
    block_rows = trailing.shape[1] // rows_size
    own_rows = lax.dynamic_slice_in_dim(all_rows, col_index * block_rows, block_rows, 0)
    picked = lax.all_gather(own_rows, "row", axis=0, tiled=True)
    update = lax.dot_general(
        all_rows, picked, (((1,), (1,)), ((), ())), preferred_element_type=F32
    )
    return (lower_slab, trailing - update)


def solution(mesh):
    return jax.shard_map(
        body,
        mesh=mesh,
        in_specs=(
            P(),
            P(),
            P(),
            P(),
            P(),
            P(("row", "col"), None),
            P(("row", "col")),
            P(("row", "col")),
            P(("row", "col")),
            P("row", "col"),
        ),
        out_specs=(P(("row", "col"), None), P("row", "col")),
        check_vma=False,
    )
```
